512 devices in a mesh: row: 16 (over x, z_hi, core), col: 32 (over z_lo, y).
Axes of the slice: x: 4, y: 4, z: 16 (z_hi: 2, z_lo: 8; z = z_hi * 8 + z_lo), core: 2. Of those that a mesh axis runs over, the one named last changes fastest.
Arguments:
- kernel: float32 [16384, 16384], P('row', 'col'), may hold values from 0 to 20, as said below
Outputs:
- factored: float32 [16384, 16384], P('row', 'col')
The draws below stay inside these ranges and needn't reach their ends.
Inputs may be any that keep to these rules, and one draw needn't show every extreme that they name: `kernel`: in logical order K is symmetric and positive definite.
All inputs are finite; a program needn't handle non-finite values.
Results may differ from the reference program's by a relative error of at most 0.0003.
Values sent between devices are 32-bit elements; how exact they have to be, the bound alone decides.
A program may use at most 64 MiB of HBM per device.

```python
import jax
import jax.numpy as jnp
from jax import lax

NB = 512
ORDER = 16384
STEPS = 1
N_ROW = 16
N_COL = 32


def draw_kernel(key, part):
    first_key, second_key = jax.random.split(key, 2)
    features = jax.random.normal(first_key, (ORDER, 16), jnp.float32)
    squares = jnp.sum(features * features, axis=1)
    inner = jnp.dot(features, features.T, precision=lax.Precision.HIGHEST)
    distance = jnp.maximum(squares[:, None] + squares[None, :] - 2.0 * inner, 0.0)
    gram = jnp.exp(distance * (-1.0 / 16.0))
    gram = 0.5 * (gram + gram.T)
    positions = jnp.arange(ORDER)
    on_diagonal = positions[:, None] == positions[None, :]
    ridge = jax.random.uniform(second_key, (ORDER,), jnp.float32, 0.05, 0.1)
    logical = jnp.where(on_diagonal, 1.0 + ridge[:, None], gram)
    block_rows = ORDER // (NB * N_ROW)
    block_cols = ORDER // (NB * N_COL)
    shaped = logical.reshape(block_rows, N_ROW, NB, block_cols, N_COL, NB)
    return shaped.transpose(1, 0, 2, 4, 3, 5).reshape(ORDER, ORDER)


def setup_inputs(seed: int = 0) -> dict:
    keys = jax.random.split(jax.random.key(seed), 2)
    return {
        "kernel": draw_kernel(jax.random.fold_in(keys[1], 71), 0),
    }


def to_logical(stored):
    block_rows = ORDER // (NB * N_ROW)
    block_cols = ORDER // (NB * N_COL)
    shaped = stored.reshape(N_ROW, block_rows, NB, N_COL, block_cols, NB)
    return shaped.transpose(1, 0, 2, 4, 3, 5).reshape(ORDER, ORDER)

def to_storage(logical):
    block_rows = ORDER // (NB * N_ROW)
    block_cols = ORDER // (NB * N_COL)
    shaped = logical.reshape(block_rows, N_ROW, NB, block_cols, N_COL, NB)
    return shaped.transpose(1, 0, 2, 4, 3, 5).reshape(ORDER, ORDER)

def reference(kernel):
    matrix = to_logical(kernel)
    for section_index in range(STEPS):
        lower_edge = section_index * NB
        upper_edge = lower_edge + NB
        factor = jnp.linalg.cholesky(matrix[lower_edge:upper_edge, lower_edge:upper_edge])
        below = matrix[upper_edge:, lower_edge:upper_edge]
        solved = jax.scipy.linalg.solve_triangular(factor, below.T, lower=True).T
        update = lax.dot_general(solved, solved, (((1,), (1,)), ((), ())), precision=lax.Precision.HIGHEST)
        matrix = matrix.at[upper_edge:, upper_edge:].set(matrix[upper_edge:, upper_edge:] - update)
        matrix = matrix.at[lower_edge:upper_edge, lower_edge:upper_edge].set(factor)
        matrix = matrix.at[upper_edge:, lower_edge:upper_edge].set(solved)
        matrix = matrix.at[lower_edge:upper_edge, upper_edge:].set(jnp.zeros_like(matrix[lower_edge:upper_edge, upper_edge:]))
    return to_storage(matrix)
```

```python
import jax
import jax.numpy as jnp
from jax import lax
from jax.experimental import pallas as pl
from jax.experimental.pallas import tpu as pltpu
from jax.sharding import PartitionSpec as P

NB = 512
B = 128
KROWS = 10 * B
UNITS = [(i, j) for i in range(4) for j in range(i, 4)]
KCH = 64
ACH = 16
NA = 1024 // ACH
F32 = jnp.float32


def comm_kernel(x_ref, kbuf, ap, aq, lsem, ksend, krecv, asend, arecv, q1s, q1r, q2s, q2r, q3s, q3r):
    r = lax.axis_index("row")
    q = lax.axis_index("col")
    x, zh, c = r // 4, (r // 2) % 2, r % 2
    zl, y = q // 4, q % 4
    z = zh * 8 + zl

    def dev(dx=0, dy=0, dz=0, dc=0):
        xx, yy, zz = (x + dx) % 4, (y + dy) % 4, (z + dz) % 16
        cc = (c + dc) % 2
        return {"row": xx * 4 + (zz // 8) * 2 + cc, "col": (zz % 8) * 4 + yy}

    group = [(dx, dc) for dx in range(4) for dc in range(2) if dx or dc]
    partners = [dict(dy=1), dict(dy=3), dict(dz=1), dict(dz=15), dict(dz=8)]
    partners += [dict(dx=dx, dc=dc) for dx, dc in group]
    barrier = pltpu.get_barrier_semaphore()
    for p in partners:
        pl.semaphore_signal(barrier, inc=1, device_id=dev(**p), device_id_type=pl.DeviceIdType.MESH)

    kroot = (r == 0) & (q == 0)
    locals_k = [
        pltpu.make_async_copy(
            x_ref.at[pl.ds(B * i, B), pl.ds(B * j, B)], kbuf.at[pl.ds(B * n, B)], lsem.at[n]
        )
        for n, (i, j) in enumerate(UNITS)
    ]
    local_a = pltpu.make_async_copy(x_ref, ap, lsem.at[10])
    local_q = pltpu.make_async_copy(x_ref.at[pl.ds(0, NB)], aq, lsem.at[11])

    @pl.when(kroot)
    def _():
        for cp in locals_k:
            cp.start()

    @pl.when(q == 0)
    def _():
        local_a.start()

    @pl.when(r == 0)
    def _():
        local_q.start()

    pl.semaphore_wait(barrier, len(partners))

    @pl.when(kroot)
    def _():
        for cp in locals_k:
            cp.wait()

    @pl.when(q == 0)
    def _():
        local_a.wait()

    @pl.when(r == 0)
    def _():
        local_q.wait()

    def remote(ref, ssem, rsem, d):
        return pltpu.make_async_remote_copy(
            src_ref=ref, dst_ref=ref, send_sem=ssem, recv_sem=rsem,
            device_id=dev(**d), device_id_type=pl.DeviceIdType.MESH,
        )

    pos = {"x": x, "y": y, "z": z}
    size = {"x": 4, "y": 4, "z": 16}
    k_trees = []
    for order in ("xyz", "yzx", "zxy"):
        children = []
        for k, d in enumerate(order):
            n = size[d]
            later = True
            for e in order[k + 1:]:
                later = later & (pos[e] == 0)
            children.append(((c == 0) & later & (pos[d] < n // 2), {"d" + d: 1}))
            children.append(
                ((c == 0) & later & ((pos[d] == 0) | (pos[d] >= n // 2 + 2)), {"d" + d: n - 1})
            )
        children.append((c == 0, {"dc": 1}))
        k_trees.append(children)

    def k_chunk(ch):
        return kbuf.at[pl.ds(KCH * ch, KCH)]

    for ch in range(KROWS // KCH):
        children = k_trees[ch % 3]

        @pl.when(jnp.logical_not(kroot))
        def _():
            remote(k_chunk(ch), ksend.at[ch, 0], krecv.at[ch], {"dc": 1}).wait_recv()

        for n, (cond, d) in enumerate(children):
            @pl.when(cond)
            def _():
                remote(k_chunk(ch), ksend.at[ch, n], krecv.at[ch], d).start()

    def q_piece(e):
        return aq.at[pl.ds(64 * e, 64)]

    mine = x * 2 + c

    @pl.when(r == 0)
    def _():
        for n, (dx, dc) in enumerate(group):
            remote(q_piece(dx * 2 + dc), q1s.at[n], q1r, dict(dx=dx, dc=dc)).start()

    @pl.when((zh == 0) & (r != 0))
    def _():
        remote(q_piece(mine), q1s.at[0], q1r, dict(dc=1)).wait_recv()

    @pl.when(zh == 0)
    def _():
        remote(q_piece(mine), q2s, q2r, dict(dz=8)).start()

    def gather(n, dx, dc):
        to_source = (zh == 0) & ((x + dx) % 4 == 0) & ((c + dc) % 2 == 0)
        return jnp.logical_not(to_source), remote(
            q_piece(mine), q3s.at[n], q3r.at[mine], dict(dx=dx, dc=dc)
        )

    @pl.when(zh == 0)
    def _():
        for n, (dx, dc) in enumerate(group):
            cond, cp = gather(n, dx, dc)

            @pl.when(cond)
            def _():
                cp.start()

    a_trees = [
        [
            ((y == 0) & (zl < 7), dict(dz=1)),
            ((y == 0) & (zl >= 1), dict(dy=1)),
            (((y == 0) | (y == 3)) & (zl >= 1), dict(dy=3)),
            ((zl == 1) & (y != 0), dict(dz=15)),
        ],
        [
            ((y == 1) & (zl < 7), dict(dz=1)),
            (((y == 0) & (zl == 0)) | (y == 1) | (y == 2), dict(dy=1)),
            ((y == 1) & (zl >= 1), dict(dy=3)),
        ],
        [
            (((y == 3) | (y == 2)) & (zl < 7), dict(dz=1)),
            ((y == 3) & (zl >= 1), dict(dy=1)),
            (((y == 0) & (zl == 0)) | ((y == 3) & (zl == 0)) | (y == 2), dict(dy=3)),
        ],
    ]

    def a_chunk(ch):
        return ap.at[pl.ds(pl.multiple_of(ACH * ch, ACH), ACH)]

    def a_step(k, carry):
        for t in range(3):
            ch = 3 * k + t

            @pl.when(ch < NA)
            def _():
                @pl.when(q != 0)
                def _():
                    remote(a_chunk(ch), asend.at[ch, 0], arecv.at[ch], dict(dy=1)).wait_recv()

                for n, (cond, d) in enumerate(a_trees[t]):
                    @pl.when(cond)
                    def _():
                        remote(a_chunk(ch), asend.at[ch, n], arecv.at[ch], d).start()

        return carry

    steps = -(-NA // 3)
    lax.fori_loop(0, steps // 2, a_step, 0)

    @pl.when(zh == 1)
    def _():
        remote(q_piece(mine), q2s, q2r, dict(dz=8)).wait_recv()
        for n, (dx, dc) in enumerate(group):
            gather(n, dx, dc)[1].start()

    lax.fori_loop(steps // 2, steps, a_step, 0)

    for n, (dx, dc) in enumerate(group):
        e = ((x + dx) % 4) * 2 + (c + dc) % 2
        cond, cp = gather(n, dx, dc)

        @pl.when(r != 0)
        def _():
            remote(q_piece(e), q3s.at[n], q3r.at[e], dict(dc=1)).wait_recv()

        @pl.when(cond)
        def _():
            cp.wait_send()

        @pl.when(r == 0)
        def _():
            remote(q_piece(dx * 2 + dc), q1s.at[n], q1r, dict(dx=dx, dc=dc)).wait_send()

    @pl.when(zh == 0)
    def _():
        remote(q_piece(mine), q2s, q2r, dict(dz=8)).wait_send()

    for ch in range(KROWS // KCH):
        for n, (cond, d) in enumerate(k_trees[ch % 3]):
            @pl.when(cond)
            def _():
                remote(k_chunk(ch), ksend.at[ch, n], krecv.at[ch], d).wait_send()

    def a_drain(k, carry):
        for t in range(3):
            ch = 3 * k + t

            @pl.when(ch < NA)
            def _():
                for n, (cond, d) in enumerate(a_trees[t]):
                    @pl.when(cond)
                    def _():
                        remote(a_chunk(ch), asend.at[ch, n], arecv.at[ch], d).wait_send()

        return carry

    lax.fori_loop(0, steps, a_drain, 0)


def distribute(kernel):
    dma = pltpu.SemaphoreType.DMA
    return pl.pallas_call(
        comm_kernel,
        out_shape=(
            jax.ShapeDtypeStruct((KROWS, B), F32),
            jax.ShapeDtypeStruct((2 * NB, NB), F32),
            jax.ShapeDtypeStruct((NB, NB), F32),
        ),
        in_specs=[pl.BlockSpec(memory_space=pl.ANY)],
        out_specs=[pl.BlockSpec(memory_space=pltpu.VMEM)] * 3,
        scratch_shapes=[
            dma((12,)),
            dma((KROWS // KCH, 7)), dma((KROWS // KCH,)),
            dma((NA, 4)), dma((NA,)),
            dma((7,)), dma(()),
            dma(()), dma(()),
            dma((7,)), dma((8,)),
        ],
        compiler_params=pltpu.CompilerParams(collective_id=0, has_side_effects=True),
        name="distribute",
    )(kernel)


def on_device(kernel):
    row = lax.axis_index("row")
    col = lax.axis_index("col")
    packed, ap, aqt = distribute(kernel)
    blocks = {u: packed[B * n : B * n + B] for n, u in enumerate(UNITS)}
    corner = jnp.concatenate(
        [
            jnp.concatenate(
                [blocks[(i, j)] if i <= j else blocks[(j, i)].T for j in range(4)], axis=1
            )
            for i in range(4)
        ],
        axis=0,
    )
    factor = jnp.linalg.cholesky(corner)
    inverse = jax.scipy.linalg.solve_triangular(factor, jnp.eye(NB, dtype=F32), lower=True)
    hi = lax.Precision.HIGHEST
    panel = jnp.dot(ap, inverse.T, precision=hi)
    piece = jnp.dot(inverse, aqt, precision=hi)
    out = kernel - jnp.dot(panel, piece, precision=hi)
    rows = jnp.arange(2 * NB)[:, None]
    top = (row == 0) & (rows < NB)
    first = jnp.where(top, jnp.tile(factor, (2, 1)), panel)
    return jnp.where(col == 0, first, jnp.where(top, 0.0, out))


def solution(mesh):
    return jax.shard_map(
        on_device, mesh=mesh, in_specs=(P("row", "col"),), out_specs=P("row", "col"), check_vma=False
    )
```

```python
import jax
import jax.numpy as jnp
from jax import lax
from jax.experimental import pallas as pl
from jax.experimental.pallas import tpu as pltpu
from jax.sharding import PartitionSpec as P

NB = 512
B = 128
KROWS = 10 * B
UNITS = [(i, j) for i in range(4) for j in range(i, 4)]
KCH = 64
ACH = 16
NA = 1024 // ACH
LAG = 3
F32 = jnp.float32


def comm_kernel(x_ref, kbuf, ap, aq, lsem, ksend, krecv, asend, arecv, q1s, q1r, q2s, q2r, q3s, q3r, tok):
    r = lax.axis_index("row")
    q = lax.axis_index("col")
    x, zh, c = r // 4, (r // 2) % 2, r % 2
    zl, y = q // 4, q % 4
    z = zh * 8 + zl

    def dev(dx=0, dy=0, dz=0, dc=0):
        xx, yy, zz = (x + dx) % 4, (y + dy) % 4, (z + dz) % 16
        cc = (c + dc) % 2
        return {"row": xx * 4 + (zz // 8) * 2 + cc, "col": (zz % 8) * 4 + yy}

    group = [(dx, dc) for dx in range(4) for dc in range(2) if dx or dc]
    partners = [dict(dy=1), dict(dy=3), dict(dz=1), dict(dz=15)]
    partners += [dict(dx=dx, dc=dc) for dx, dc in group]
    barrier = pltpu.get_barrier_semaphore()
    for p in partners:
        pl.semaphore_signal(barrier, inc=1, device_id=dev(**p), device_id_type=pl.DeviceIdType.MESH)

    kroot = (r == 0) & (q == 0)
    locals_k = [
        pltpu.make_async_copy(
            x_ref.at[pl.ds(B * i, B), pl.ds(B * j, B)], kbuf.at[pl.ds(B * n, B)], lsem.at[n]
        )
        for n, (i, j) in enumerate(UNITS)
    ]
    local_a = pltpu.make_async_copy(x_ref, ap, lsem.at[10])
    local_q = pltpu.make_async_copy(x_ref.at[pl.ds(0, NB)], aq, lsem.at[11])

    @pl.when(kroot)
    def _():
        for cp in locals_k:
            cp.start()

    @pl.when(q == 0)
    def _():
        local_a.start()

    @pl.when(r == 0)
    def _():
        local_q.start()

    pl.semaphore_wait(barrier, len(partners))

    @pl.when(kroot)
    def _():
        for cp in locals_k:
            cp.wait()

    @pl.when(q == 0)
    def _():
        local_a.wait()

    @pl.when(r == 0)
    def _():
        local_q.wait()

    def remote(ref, ssem, rsem, d):
        return pltpu.make_async_remote_copy(
            src_ref=ref, dst_ref=ref, send_sem=ssem, recv_sem=rsem,
            device_id=dev(**d), device_id_type=pl.DeviceIdType.MESH,
        )

    pos = {"x": x, "y": y, "z": z}
    size = {"x": 4, "y": 4, "z": 16}
    k_trees = []
    for order in ("xyz", "yzx", "zxy"):
        children = []
        for k, d in enumerate(order):
            n = size[d]
            later = True
            for e in order[k + 1:]:
                later = later & (pos[e] == 0)
            children.append(((c == 0) & later & (pos[d] < n // 2), {"d" + d: 1}))
            children.append(
                ((c == 0) & later & ((pos[d] == 0) | (pos[d] >= n // 2 + 2)), {"d" + d: n - 1})
            )
        children.append((c == 0, {"dc": 1}))
        k_trees.append(children)

    def k_chunk(ch):
        return kbuf.at[pl.ds(KCH * ch, KCH)]

    for ch in range(KROWS // KCH):
        children = k_trees[ch % 3]

        @pl.when(jnp.logical_not(kroot))
        def _():
            remote(k_chunk(ch), ksend.at[ch, 0], krecv.at[ch], {"dc": 1}).wait_recv()

        for n, (cond, d) in enumerate(children):
            @pl.when(cond)
            def _():
                remote(k_chunk(ch), ksend.at[ch, n], krecv.at[ch], d).start()

    def q_piece(e):
        return aq.at[pl.ds(64 * e, 64)]

    mine = x * 2 + c

    @pl.when(r == 0)
    def _():
        for n, (dx, dc) in enumerate(group):
            remote(q_piece(dx * 2 + dc), q1s.at[n], q1r, dict(dx=dx, dc=dc)).start()

    @pl.when((zh == 0) & (r != 0))
    def _():
        remote(q_piece(mine), q1s.at[0], q1r, dict(dc=1)).wait_recv()

    for n in range(8):
        if n:
            pl.semaphore_wait(tok.at[n - 1], 1)
        pl.semaphore_signal(
            tok.at[n], inc=1, device_id=dev(dz=15), device_id_type=pl.DeviceIdType.MESH
        )
    pl.semaphore_wait(tok.at[7], 1)

    @pl.when(zh == 0)
    def _():
        remote(q_piece(mine), q2s, q2r, dict(dz=8)).start()

    def gather(n, dx, dc):
        to_source = (zh == 0) & ((x + dx) % 4 == 0) & ((c + dc) % 2 == 0)
        return jnp.logical_not(to_source), remote(
            q_piece(mine), q3s.at[n], q3r.at[mine], dict(dx=dx, dc=dc)
        )

    @pl.when(zh == 0)
    def _():
        for n, (dx, dc) in enumerate(group):
            cond, cp = gather(n, dx, dc)

            @pl.when(cond)
            def _():
                cp.start()

    a_trees = [
        [
            ((y == 0) & (zl < 7), dict(dz=1)),
            ((y == 0) & (zl >= 1), dict(dy=1)),
            (((y == 0) | (y == 3)) & (zl >= 1), dict(dy=3)),
            ((zl == 1) & (y != 0), dict(dz=15)),
        ],
        [
            ((y == 1) & (zl < 7), dict(dz=1)),
            (((y == 0) & (zl == 0)) | (y == 1) | (y == 2), dict(dy=1)),
            ((y == 1) & (zl >= 1), dict(dy=3)),
        ],
        [
            (((y == 3) | (y == 2)) & (zl < 7), dict(dz=1)),
            ((y == 3) & (zl >= 1), dict(dy=1)),
            (((y == 0) & (zl == 0)) | ((y == 3) & (zl == 0)) | (y == 2), dict(dy=3)),
        ],
    ]

    def a_chunk(ch):
        return ap.at[pl.ds(pl.multiple_of(ACH * ch, ACH), ACH)]

    def pick(options):
        value = options[-1][1]
        for cond, v in reversed(options[:-1]):
            value = jnp.where(cond, v, value)
        return value

    depths = [
        pick([((y == 0), zl), ((zl == 0) & (y == 2), 4), (zl == 0, 3), (y == 2, zl + 2), (True, zl + 1)]),
        pick([((y == 0) & (zl == 0), 0), (y == 1, zl + 1), (y == 3, zl + 3), (True, zl + 2)]),
        pick([((y == 0) & (zl == 0), 0), (y == 3, zl + 1), (y == 1, zl + 3), (True, zl + 2)]),
    ]

    def a_step(g, carry):
        for t in range(3):
            k = g - LAG * depths[t]
            ch = 3 * k + t

            @pl.when((k >= 0) & (ch < NA))
            def _():
                @pl.when(q != 0)
                def _():
                    remote(a_chunk(ch), asend.at[ch, 0], arecv.at[ch], dict(dy=1)).wait_recv()

                for n, (cond, d) in enumerate(a_trees[t]):
                    @pl.when(cond)
                    def _():
                        remote(a_chunk(ch), asend.at[ch, n], arecv.at[ch], d).start()

        return carry

    chunks = -(-NA // 3)
    steps = chunks + 10 * LAG
    lax.fori_loop(0, steps // 2, a_step, 0)

    @pl.when(zh == 1)
    def _():
        remote(q_piece(mine), q2s, q2r, dict(dz=8)).wait_recv()
        for n, (dx, dc) in enumerate(group):
            gather(n, dx, dc)[1].start()

    lax.fori_loop(steps // 2, steps, a_step, 0)

    for n, (dx, dc) in enumerate(group):
        e = ((x + dx) % 4) * 2 + (c + dc) % 2
        cond, cp = gather(n, dx, dc)

        @pl.when(r != 0)
        def _():
            remote(q_piece(e), q3s.at[n], q3r.at[e], dict(dc=1)).wait_recv()

        @pl.when(cond)
        def _():
            cp.wait_send()

        @pl.when(r == 0)
        def _():
            remote(q_piece(dx * 2 + dc), q1s.at[n], q1r, dict(dx=dx, dc=dc)).wait_send()

    @pl.when(zh == 0)
    def _():
        remote(q_piece(mine), q2s, q2r, dict(dz=8)).wait_send()

    for ch in range(KROWS // KCH):
        for n, (cond, d) in enumerate(k_trees[ch % 3]):
            @pl.when(cond)
            def _():
                remote(k_chunk(ch), ksend.at[ch, n], krecv.at[ch], d).wait_send()

    def a_drain(k, carry):
        for t in range(3):
            ch = 3 * k + t

            @pl.when(ch < NA)
            def _():
                for n, (cond, d) in enumerate(a_trees[t]):
                    @pl.when(cond)
                    def _():
                        remote(a_chunk(ch), asend.at[ch, n], arecv.at[ch], d).wait_send()

        return carry

    lax.fori_loop(0, chunks, a_drain, 0)


def distribute(kernel):
    dma = pltpu.SemaphoreType.DMA
    return pl.pallas_call(
        comm_kernel,
        out_shape=(
            jax.ShapeDtypeStruct((KROWS, B), F32),
            jax.ShapeDtypeStruct((2 * NB, NB), F32),
            jax.ShapeDtypeStruct((NB, NB), F32),
        ),
        in_specs=[pl.BlockSpec(memory_space=pl.ANY)],
        out_specs=[pl.BlockSpec(memory_space=pltpu.VMEM)] * 3,
        scratch_shapes=[
            dma((12,)),
            dma((KROWS // KCH, 7)), dma((KROWS // KCH,)),
            dma((NA, 4)), dma((NA,)),
            dma((7,)), dma(()),
            dma(()), dma(()),
            dma((7,)), dma((8,)),
            pltpu.SemaphoreType.REGULAR((8,)),
        ],
        compiler_params=pltpu.CompilerParams(collective_id=0, has_side_effects=True),
        name="distribute",
    )(kernel)


HI = lax.Precision.HIGHEST


def lane(v, k):
    return jnp.take_along_axis(v, jnp.full((8, B), k, jnp.int32), axis=1)

def sub(v, i):
    return jnp.broadcast_to(v[i:i + 1, :], (8, B))

def micro(d, e):
    n = len(d)
    iota = lax.broadcasted_iota(jnp.int32, (8, B), 0)
    us, vs = [], []
    for s in range(n):
        j0 = 8 * s
        cols = [lane(d[s], j0 + k) for k in range(8)]
        sp = {(i, k): sub(cols[k], i) for k in range(8) for i in range(k + 1)}
        m = {}
        rec = []
        mcol = []
        dvec = sp[0, 0]
        for j in range(8):
            r = 1.0 / sp[j, j]
            rec.append(r)
            if j:
                dvec = jnp.where(iota == j, sp[j, j], dvec)
            f = {i: sp[j, i] * r for i in range(j + 1, 8)}
            fv = jnp.where(iota > j, cols[j] * r, 0.0)
            for k in range(j + 1, 8):
                cols[k] = cols[k] - fv * sp[j, k]
            for k in range(j):
                mcol[k] = mcol[k] - fv * m[j, k]
            mcol.append(jnp.where(iota == j, 1.0, -fv))
            for i in range(j + 1, 8):
                for k in range(i, 8):
                    sp[i, k] = sp[i, k] - f[i] * sp[j, k]
                for k in range(j):
                    m[i, k] = m[i, k] - f[i] * m[j, k]
                m[i, j] = -f[i]
        def apply(v):
            t = [mcol[k] * sub(v, k) for k in range(8)]
            while len(t) > 1:
                t = [t[i] + t[i + 1] for i in range(0, len(t), 2)]
            return t[0]
        z, w = apply(d[s]), apply(e[s])
        rs = lax.rsqrt(dvec)
        us.append(z * rs)
        vs.append(w * rs)
        zr = [sub(z, k) * rec[k] for k in range(8)]
        wr = [sub(w, k) * rec[k] for k in range(8)]
        for t in range(s + 1, n):
            qs = [lane(d[t], j0 + k) for k in range(8)]
            for k in range(8):
                yk = qs[k]
                for l in range(k):
                    yk = yk + m[k, l] * qs[l]
                d[t] = d[t] - yk * zr[k]
                e[t] = e[t] - yk * wr[k]
    return us, vs

def dot(a, b):
    return jnp.dot(a, b, precision=HI, preferred_element_type=F32)


def dot_t(a, b):
    return lax.dot_general(a, b, (((1,), (1,)), ((), ())), precision=HI, preferred_element_type=F32)


def tdot(a, b):
    return lax.dot_general(a, b, (((0,), (0,)), ((), ())), precision=HI, preferred_element_type=F32)

def factor(k_ref, u_ref, x_ref, w_ref):
    for n, (i, j) in enumerate(UNITS):
        w_ref[B * i:B * i + B, B * j:B * j + B] = k_ref[B * n:B * n + B, :]
    x_ref[...] = jnp.zeros((NB, NB), F32)
    u_ref[...] = jnp.zeros((NB, NB), F32)
    row = lax.broadcasted_iota(jnp.int32, (8, B), 0)
    col = lax.broadcasted_iota(jnp.int32, (8, B), 1)
    for k in range(4):
        o = B * k
        d = [w_ref[o + 8 * t:o + 8 * t + 8, o:o + B] for t in range(16)]
        e = [jnp.where(col == row + 8 * t, 1.0, 0.0) for t in range(16)]
        us, vs = micro(d, e)
        for t in range(16):
            u_ref[o + 8 * t:o + 8 * t + 8, o:o + B] = jnp.where(col >= row + 8 * t, us[t], 0.0)
            x_ref[o + 8 * t:o + 8 * t + 8, o:o + B] = vs[t]
        li = x_ref[o:o + B, o:o + B]
        if k:
            x_ref[o:o + B, :o] = jnp.dot(li, x_ref[o:o + B, :o], precision=HI, preferred_element_type=F32)
        if k < 3:
            u = jnp.dot(li, w_ref[o:o + B, o + B:], precision=HI, preferred_element_type=F32)
            u_ref[o:o + B, o + B:] = u
            w_ref[o + B:, o + B:] = w_ref[o + B:, o + B:] - tdot(u, u)
            x_ref[o + B:, :o + B] = x_ref[o + B:, :o + B] - tdot(u, x_ref[o:o + B, :o + B])


def update_kernel(k_any, a_any, q_any, g_any, o_ref, kbuf, ap, aq, u_ref, x_ref, w_ref, pq, sems):
    r = lax.axis_index("row")
    q = lax.axis_index("col")
    loads = [
        pltpu.make_async_copy(src, dst, sems.at[n])
        for n, (src, dst) in enumerate([(k_any, kbuf), (a_any, ap), (q_any, aq), (g_any, o_ref)])
    ]
    for cp in loads:
        cp.start()
    loads[0].wait()
    factor(kbuf, u_ref, x_ref, w_ref)
    loads[1].wait()
    loads[2].wait()
    loads[3].wait()

    half = NB // 2
    pq[:half] = dot(x_ref[:half, :half], aq[:half, :])
    pq[half:] = dot(x_ref[half:, :], aq[...])
    rows = 256

    def body(n, carry):
        sl = pl.ds(pl.multiple_of(rows * n, rows), rows)
        a = ap[sl, :]
        p = jnp.concatenate(
            [dot_t(a[:, :half], x_ref[:half, :half]), dot_t(a, x_ref[half:, :])], axis=1
        )

        @pl.when(q == 0)
        def _():
            o_ref[sl, :] = p

        @pl.when(q != 0)
        def _():
            o_ref[sl, :] = o_ref[sl, :] - dot(p, pq[...])

        return carry

    lax.fori_loop(0, 2 * NB // rows, body, 0)

    @pl.when(r == 0)
    def _():
        @pl.when(q == 0)
        def _():
            for i in range(4):
                for j in range(4):
                    o_ref[B * i:B * i + B, B * j:B * j + B] = u_ref[B * j:B * j + B, B * i:B * i + B].T

        @pl.when(q != 0)
        def _():
            o_ref[:NB, :] = jnp.zeros((NB, NB), F32)


def update(kbuf, ap, aq, kernel):
    vmem = pltpu.VMEM
    return pl.pallas_call(
        update_kernel,
        out_shape=jax.ShapeDtypeStruct((2 * NB, NB), F32),
        in_specs=[pl.BlockSpec(memory_space=pl.ANY)] * 4,
        out_specs=pl.BlockSpec(memory_space=vmem),
        scratch_shapes=[
            vmem((KROWS, B), F32), vmem((2 * NB, NB), F32), vmem((NB, NB), F32),
            vmem((NB, NB), F32), vmem((NB, NB), F32), vmem((NB, NB), F32), vmem((NB, NB), F32),
            pltpu.SemaphoreType.DMA((4,)),
        ],
        name="update",
    )(kbuf, ap, aq, kernel)


def on_device(kernel):
    kbuf, ap, aq = distribute(kernel)
    return update(kbuf, ap, aq, kernel)


def solution(mesh):
    return jax.shard_map(
        on_device, mesh=mesh, in_specs=(P("row", "col"),), out_specs=P("row", "col"), check_vma=False
    )
```

```python
import jax
import jax.numpy as jnp
from jax import lax
from jax.experimental import pallas as pl
from jax.experimental.pallas import tpu as pltpu
from jax.sharding import PartitionSpec as P

NB = 512
B = 128
KROWS = 10 * B
UNITS = [(i, j) for i in range(4) for j in range(i, 4)]
KCH = 64
ACH = 32
NA = 1024 // ACH
LAG = 4
TOKEN, CROSS, LAND = 7, 15, 28
EARLY, FIRST = 14, 30
F32 = jnp.float32


HI = lax.Precision.HIGHEST


def lane(v, k):
    return jnp.take_along_axis(v, jnp.full((8, B), k, jnp.int32), axis=1)

def sub(v, i):
    return jnp.broadcast_to(v[i:i + 1, :], (8, B))

def micro(d, e):
    n = len(d)
    iota = lax.broadcasted_iota(jnp.int32, (8, B), 0)
    us, vs = [], []
    for s in range(n):
        j0 = 8 * s
        cols = [lane(d[s], j0 + k) for k in range(8)]
        sp = {(i, k): sub(cols[k], i) for k in range(8) for i in range(k + 1)}
        m = {}
        rec = []
        mcol = []
        dvec = sp[0, 0]
        for j in range(8):
            r = 1.0 / sp[j, j]
            rec.append(r)
            if j:
                dvec = jnp.where(iota == j, sp[j, j], dvec)
            f = {i: sp[j, i] * r for i in range(j + 1, 8)}
            fv = jnp.where(iota > j, cols[j] * r, 0.0)
            for k in range(j + 1, 8):
                cols[k] = cols[k] - fv * sp[j, k]
            for k in range(j):
                mcol[k] = mcol[k] - fv * m[j, k]
            mcol.append(jnp.where(iota == j, 1.0, -fv))
            for i in range(j + 1, 8):
                for k in range(i, 8):
                    sp[i, k] = sp[i, k] - f[i] * sp[j, k]
                for k in range(j):
                    m[i, k] = m[i, k] - f[i] * m[j, k]
                m[i, j] = -f[i]
        def apply(v):
            t = [mcol[k] * sub(v, k) for k in range(8)]
            while len(t) > 1:
                t = [t[i] + t[i + 1] for i in range(0, len(t), 2)]
            return t[0]
        z, w = apply(d[s]), apply(e[s])
        rs = lax.rsqrt(dvec)
        us.append(z * rs)
        vs.append(w * rs)
        zr = [sub(z, k) * rec[k] for k in range(8)]
        wr = [sub(w, k) * rec[k] for k in range(8)]
        for t in range(s + 1, n):
            qs = [lane(d[t], j0 + k) for k in range(8)]
            for k in range(8):
                yk = qs[k]
                for l in range(k):
                    yk = yk + m[k, l] * qs[l]
                d[t] = d[t] - yk * zr[k]
                e[t] = e[t] - yk * wr[k]
    return us, vs

def dot(a, b):
    return jnp.dot(a, b, precision=HI, preferred_element_type=F32)


def dot_t(a, b):
    return lax.dot_general(a, b, (((1,), (1,)), ((), ())), precision=HI, preferred_element_type=F32)


def tdot(a, b):
    return lax.dot_general(a, b, (((0,), (0,)), ((), ())), precision=HI, preferred_element_type=F32)

def factor(k_ref, u_ref, x_ref, w_ref):
    for n, (i, j) in enumerate(UNITS):
        w_ref[B * i:B * i + B, B * j:B * j + B] = k_ref[B * n:B * n + B, :]
    x_ref[...] = jnp.zeros((NB, NB), F32)
    u_ref[...] = jnp.zeros((NB, NB), F32)
    row = lax.broadcasted_iota(jnp.int32, (8, B), 0)
    col = lax.broadcasted_iota(jnp.int32, (8, B), 1)
    for k in range(4):
        o = B * k
        d = [w_ref[o + 8 * t:o + 8 * t + 8, o:o + B] for t in range(16)]
        e = [jnp.where(col == row + 8 * t, 1.0, 0.0) for t in range(16)]
        us, vs = micro(d, e)
        for t in range(16):
            u_ref[o + 8 * t:o + 8 * t + 8, o:o + B] = jnp.where(col >= row + 8 * t, us[t], 0.0)
            x_ref[o + 8 * t:o + 8 * t + 8, o:o + B] = vs[t]
        li = x_ref[o:o + B, o:o + B]
        if k:
            x_ref[o:o + B, :o] = jnp.dot(li, x_ref[o:o + B, :o], precision=HI, preferred_element_type=F32)
        if k < 3:
            u = jnp.dot(li, w_ref[o:o + B, o + B:], precision=HI, preferred_element_type=F32)
            u_ref[o:o + B, o + B:] = u
            w_ref[o + B:, o + B:] = w_ref[o + B:, o + B:] - tdot(u, u)
            x_ref[o + B:, :o + B] = x_ref[o + B:, :o + B] - tdot(u, x_ref[o:o + B, :o + B])


def comm_kernel(
    g_ref, k_out, ap_out, aq_out, kbuf, ap, aq,
    lsem, ksend, krecv, asend, arecv, q1s, q1r, q2s, q2r, q3s, q3r, tok,
):
    r = lax.axis_index("row")
    q = lax.axis_index("col")
    x, zh, c = r // 4, (r // 2) % 2, r % 2
    zl, y = q // 4, q % 4
    z = zh * 8 + zl

    def dev(dx=0, dy=0, dz=0, dc=0):
        xx, yy, zz = (x + dx) % 4, (y + dy) % 4, (z + dz) % 16
        cc = (c + dc) % 2
        return {"row": xx * 4 + (zz // 8) * 2 + cc, "col": (zz % 8) * 4 + yy}

    ids = {}

    def near(**d):
        key = tuple(sorted((k, v) for k, v in d.items() if v))
        if key not in ids:
            ids[key] = dev(**d)
        return ids[key]

    group = [(dx, dc) for dx in range(4) for dc in range(2) if dx or dc]
    partners = [dict(dy=1), dict(dy=2), dict(dy=3), dict(dz=1), dict(dz=2), dict(dz=14), dict(dz=15)]
    partners += [dict(dx=dx, dc=dc) for dx, dc in group]
    for p in partners + [dict(dz=8)]:
        near(**p)
    barrier = pltpu.get_barrier_semaphore()
    for p in partners:
        pl.semaphore_signal(barrier, inc=1, device_id=near(**p), device_id_type=pl.DeviceIdType.MESH)

    kroot = (r == 0) & (q == 0)
    locals_k = [
        pltpu.make_async_copy(
            g_ref.at[pl.ds(B * i, B), pl.ds(B * j, B)], kbuf.at[pl.ds(B * n, B)], lsem.at[n]
        )
        for n, (i, j) in enumerate(UNITS)
    ]
    local_a = pltpu.make_async_copy(g_ref, ap, lsem.at[10])
    local_q = pltpu.make_async_copy(g_ref.at[pl.ds(0, NB)], aq, lsem.at[11])

    @pl.when(kroot)
    def _():
        for cp in locals_k:
            cp.start()

    @pl.when(q == 0)
    def _():
        local_a.start()

    @pl.when(r == 0)
    def _():
        local_q.start()

    pl.semaphore_wait(barrier, len(partners))

    @pl.when(kroot)
    def _():
        for cp in locals_k:
            cp.wait()

    @pl.when(q == 0)
    def _():
        local_a.wait()

    @pl.when(r == 0)
    def _():
        local_q.wait()

    def remote(ref, ssem, rsem, d):
        return pltpu.make_async_remote_copy(
            src_ref=ref, dst_ref=ref, send_sem=ssem, recv_sem=rsem,
            device_id=near(**d), device_id_type=pl.DeviceIdType.MESH,
        )

    pos = {"x": x, "y": y, "z": z}
    k_trees = []
    for order in ("xyz", "yzx", "zxy"):
        children = []
        for k, d in enumerate(order):
            head = c == 0
            for e in order[k + 1:]:
                head = head & (pos[e] == 0)
            v = pos[d]
            if d == "z":
                even = head & (v % 2 == 0)
                children.append((even & (v < 8), dict(dz=2)))
                children.append((even & (v < 8), dict(dz=1)))
                children.append((even & ((v == 0) | (v > 10)), dict(dz=14)))
                children.append((even & ((v == 0) | (v > 8)), dict(dz=15)))
            else:
                children += [(head & (v == 0), {"d" + d: n}) for n in (2, 1, 3)]
        children.append((c == 0, {"dc": 1}))
        k_trees.append(children)

    def k_chunk(ch):
        return kbuf.at[pl.ds(KCH * ch, KCH)]

    def k_round(s):
        for t in range(3):
            ch = 3 * s + t
            if ch >= KROWS // KCH:
                continue

            @pl.when(jnp.logical_not(kroot))
            def _():
                remote(k_chunk(ch), ksend.at[ch, 0], krecv.at[ch], {"dc": 1}).wait_recv()

            for n, (cond, d) in enumerate(k_trees[t]):
                @pl.when(cond)
                def _():
                    remote(k_chunk(ch), ksend.at[ch, n], krecv.at[ch], d).start()

    def q_piece(e):
        return aq.at[pl.ds(64 * e, 64)]

    mine = x * 2 + c

    @pl.when(r == 0)
    def _():
        for n, (dx, dc) in enumerate(group):
            remote(q_piece(dx * 2 + dc), q1s.at[n], q1r, dict(dx=dx, dc=dc)).start()

    def gather(n, dx, dc):
        to_source = (zh == 0) & ((x + dx) % 4 == 0) & ((c + dc) % 2 == 0)
        return jnp.logical_not(to_source), remote(
            q_piece(mine), q3s.at[n], q3r.at[mine], dict(dx=dx, dc=dc)
        )

    def q_cross():
        @pl.when(r != 0)
        def _():
            remote(q_piece(mine), q1s.at[0], q1r, dict(dc=1)).wait_recv()

        pl.semaphore_wait(tok.at[7], 1)
        remote(q_piece(mine), q2s, q2r, dict(dz=8)).start()
        for n, (dx, dc) in enumerate(group):
            cond, cp = gather(n, dx, dc)

            @pl.when(cond)
            def _():
                cp.start()

    def q_land():
        pl.semaphore_wait(tok.at[7], 1)
        remote(q_piece(mine), q2s, q2r, dict(dz=8)).wait_recv()
        for n, (dx, dc) in enumerate(group):
            gather(n, dx, dc)[1].start()

    def token(n):
        @pl.when(n > 0)
        def _():
            pl.semaphore_wait(tok.at[jnp.maximum(n - 1, 0)], 1)

        pl.semaphore_signal(
            tok.at[n], inc=1, device_id=near(dz=15), device_id_type=pl.DeviceIdType.MESH
        )

    a_trees = [
        [
            ((y == 0) & (zl < 7), dict(dz=1)),
            ((y == 0) & (zl >= 1), dict(dy=1)),
            (((y == 0) | (y == 3)) & (zl >= 1), dict(dy=3)),
            ((zl == 1) & (y != 0), dict(dz=15)),
        ],
        [
            ((y == 1) & (zl < 7), dict(dz=1)),
            (((y == 0) & (zl == 0)) | (y == 1) | (y == 2), dict(dy=1)),
            ((y == 1) & (zl >= 1), dict(dy=3)),
        ],
        [
            (((y == 3) | (y == 2)) & (zl < 7), dict(dz=1)),
            ((y == 3) & (zl >= 1), dict(dy=1)),
            (((y == 0) & (zl == 0)) | ((y == 3) & (zl == 0)) | (y == 2), dict(dy=3)),
        ],
    ]

    def a_chunk(ch):
        return ap.at[pl.ds(pl.multiple_of(ACH * ch, ACH), ACH)]

    def pick(options):
        value = options[-1][1]
        for cond, v in reversed(options[:-1]):
            value = jnp.where(cond, v, value)
        return value

    depths = [
        pick([((y == 0), zl), ((zl == 0) & (y == 2), 4), (zl == 0, 3), (y == 2, zl + 2), (True, zl + 1)]),
        pick([((y == 0) & (zl == 0), 0), (y == 1, zl + 1), (y == 3, zl + 3), (True, zl + 2)]),
        pick([((y == 0) & (zl == 0), 0), (y == 3, zl + 1), (y == 1, zl + 3), (True, zl + 2)]),
    ]

    def a_step(g, carry):
        for t in range(3):
            k = g - LAG * depths[t]
            ch = 3 * k + t

            @pl.when((k >= 0) & (ch < NA))
            def _():
                @pl.when(q != 0)
                def _():
                    remote(a_chunk(ch), asend.at[ch, 0], arecv.at[ch], dict(dy=1)).wait_recv()

                for n, (cond, d) in enumerate(a_trees[t]):
                    @pl.when(cond)
                    def _():
                        remote(a_chunk(ch), asend.at[ch, n], arecv.at[ch], d).start()

        @pl.when((g >= TOKEN) & (g < TOKEN + 8))
        def _():
            token(g - TOKEN)

        @pl.when((g == CROSS) & (zh == 0))
        def _():
            q_cross()

        @pl.when((g == LAND) & (zh == 1))
        def _():
            q_land()

        return carry

    chunks = -(-NA // 3)
    steps = max(chunks + 10 * LAG, LAND + 1)
    far = jnp.minimum(x, 4 - x) + jnp.minimum(y, 4 - y) + jnp.minimum(z, 16 - z)
    early = FIRST + (far * EARLY) // 8
    lax.fori_loop(0, early, a_step, 0)
    rounds = -(-(KROWS // KCH) // 3)
    for s in range(rounds):
        k_round(s)
        a_step(early + s, 0)

    lax.fori_loop(early + rounds, steps, a_step, 0)

    for n, (dx, dc) in enumerate(group):
        e = ((x + dx) % 4) * 2 + (c + dc) % 2
        cond, cp = gather(n, dx, dc)

        @pl.when(r != 0)
        def _():
            remote(q_piece(e), q3s.at[n], q3r.at[e], dict(dc=1)).wait_recv()

        @pl.when(cond)
        def _():
            cp.wait_send()

        @pl.when(r == 0)
        def _():
            remote(q_piece(dx * 2 + dc), q1s.at[n], q1r, dict(dx=dx, dc=dc)).wait_send()

    @pl.when(zh == 0)
    def _():
        remote(q_piece(mine), q2s, q2r, dict(dz=8)).wait_send()

    for ch in range(KROWS // KCH):
        for n, (cond, d) in enumerate(k_trees[ch % 3]):
            @pl.when(cond)
            def _():
                remote(k_chunk(ch), ksend.at[ch, n], krecv.at[ch], d).wait_send()

    def a_drain(k, carry):
        for t in range(3):
            ch = 3 * k + t

            @pl.when(ch < NA)
            def _():
                for n, (cond, d) in enumerate(a_trees[t]):
                    @pl.when(cond)
                    def _():
                        remote(a_chunk(ch), asend.at[ch, n], arecv.at[ch], d).wait_send()

        return carry

    lax.fori_loop(0, chunks, a_drain, 0)

    outs = [
        pltpu.make_async_copy(src, dst, lsem.at[n])
        for n, (src, dst) in enumerate([(kbuf, k_out), (ap, ap_out), (aq, aq_out)])
    ]
    for cp in outs:
        cp.start()
    for cp in outs:
        cp.wait()


def distribute(kernel):
    dma, vmem = pltpu.SemaphoreType.DMA, pltpu.VMEM
    square = (NB, NB)
    return pl.pallas_call(
        comm_kernel,
        out_shape=[
            jax.ShapeDtypeStruct((KROWS, B), F32),
            jax.ShapeDtypeStruct((2 * NB, NB), F32),
            jax.ShapeDtypeStruct(square, F32),
        ],
        in_specs=[pl.BlockSpec(memory_space=pl.ANY)],
        out_specs=[pl.BlockSpec(memory_space=pl.ANY)] * 3,
        scratch_shapes=[
            vmem((KROWS, B), F32), vmem((2 * NB, NB), F32), vmem(square, F32),
            dma((12,)),
            dma((KROWS // KCH, 11)), dma((KROWS // KCH,)),
            dma((NA, 4)), dma((NA,)),
            dma((7,)), dma(()),
            dma(()), dma(()),
            dma((7,)), dma((8,)),
            pltpu.SemaphoreType.REGULAR((8,)),
        ],
        compiler_params=pltpu.CompilerParams(collective_id=0, has_side_effects=True),
        name="distribute",
    )(kernel)


def update_kernel(k_any, a_any, q_any, g_any, o_ref, kbuf, ap, aq, u_ref, x_ref, w_ref, pq, sems):
    r = lax.axis_index("row")
    q = lax.axis_index("col")
    loads = [
        pltpu.make_async_copy(src, dst, sems.at[n])
        for n, (src, dst) in enumerate([(k_any, kbuf), (a_any, ap), (q_any, aq), (g_any, o_ref)])
    ]
    for cp in loads:
        cp.start()
    loads[0].wait()
    factor(kbuf, u_ref, x_ref, w_ref)
    loads[1].wait()
    loads[2].wait()
    loads[3].wait()

    half = NB // 2
    pq[:half] = dot(x_ref[:half, :half], aq[:half, :])
    pq[half:] = dot(x_ref[half:, :], aq[...])
    rows = 256

    def body(n, carry):
        sl = pl.ds(pl.multiple_of(rows * n, rows), rows)
        a = ap[sl, :]
        p = jnp.concatenate(
            [dot_t(a[:, :half], x_ref[:half, :half]), dot_t(a, x_ref[half:, :])], axis=1
        )

        @pl.when(q == 0)
        def _():
            o_ref[sl, :] = p

        @pl.when(q != 0)
        def _():
            o_ref[sl, :] = o_ref[sl, :] - dot(p, pq[...])

        return carry

    lax.fori_loop(0, 2 * NB // rows, body, 0)

    @pl.when(r == 0)
    def _():
        @pl.when(q == 0)
        def _():
            for i in range(4):
                for j in range(4):
                    o_ref[B * i:B * i + B, B * j:B * j + B] = u_ref[B * j:B * j + B, B * i:B * i + B].T

        @pl.when(q != 0)
        def _():
            o_ref[:NB, :] = jnp.zeros((NB, NB), F32)


def update(kbuf, ap, aq, kernel):
    vmem = pltpu.VMEM
    return pl.pallas_call(
        update_kernel,
        out_shape=jax.ShapeDtypeStruct((2 * NB, NB), F32),
        in_specs=[pl.BlockSpec(memory_space=pl.ANY)] * 4,
        out_specs=pl.BlockSpec(memory_space=vmem),
        scratch_shapes=[
            vmem((KROWS, B), F32), vmem((2 * NB, NB), F32), vmem((NB, NB), F32),
            vmem((NB, NB), F32), vmem((NB, NB), F32), vmem((NB, NB), F32), vmem((NB, NB), F32),
            pltpu.SemaphoreType.DMA((4,)),
        ],
        name="update",
    )(kbuf, ap, aq, kernel)


def on_device(kernel):
    kbuf, ap, aq = distribute(kernel)
    return update(kbuf, ap, aq, kernel)


def solution(mesh):
    return jax.shard_map(
        on_device, mesh=mesh, in_specs=(P("row", "col"),), out_specs=P("row", "col"), check_vma=False
    )
```

```python
import jax
import jax.numpy as jnp
from jax import lax
from jax.experimental import pallas as pl
from jax.experimental.pallas import tpu as pltpu
from jax.sharding import PartitionSpec as P

NB = 512
B = 128
KROWS = 10 * B
UNITS = [(i, j) for i in range(4) for j in range(i, 4)]
KCH = 64
ACH = 32
NA = 1024 // ACH
LAG = 4
TOKEN, CROSS, LAND = 7, 15, 28
EARLY, FIRST = 14, 30
F32 = jnp.float32


HI = lax.Precision.HIGHEST


def lane(v, k):
    return jnp.take_along_axis(v, jnp.full((8, B), k, jnp.int32), axis=1)

def sub(v, i):
    return jnp.broadcast_to(v[i:i + 1, :], (8, B))

def micro(d, e, beside):
    n = len(d)
    iota = lax.broadcasted_iota(jnp.int32, (8, B), 0)
    us, vs = [], []
    for s in range(n):
        beside(s)
        j0 = 8 * s
        cols = [lane(d[s], j0 + k) for k in range(8)]
        sp = {(i, k): sub(cols[k], i) for k in range(8) for i in range(k + 1)}
        m = {}
        rec = []
        mcol = []
        dvec = sp[0, 0]
        for j in range(8):
            r = 1.0 / sp[j, j]
            rec.append(r)
            if j:
                dvec = jnp.where(iota == j, sp[j, j], dvec)
            f = {i: sp[j, i] * r for i in range(j + 1, 8)}
            fv = jnp.where(iota > j, cols[j] * r, 0.0)
            for k in range(j + 1, 8):
                cols[k] = cols[k] - fv * sp[j, k]
            for k in range(j):
                mcol[k] = mcol[k] - fv * m[j, k]
            mcol.append(jnp.where(iota == j, 1.0, -fv))
            for i in range(j + 1, 8):
                for k in range(i, 8):
                    sp[i, k] = sp[i, k] - f[i] * sp[j, k]
                for k in range(j):
                    m[i, k] = m[i, k] - f[i] * m[j, k]
                m[i, j] = -f[i]
        def apply(v):
            t = [mcol[k] * sub(v, k) for k in range(8)]
            while len(t) > 1:
                t = [t[i] + t[i + 1] for i in range(0, len(t), 2)]
            return t[0]
        z, w = apply(d[s]), apply(e[s])
        rs = lax.rsqrt(dvec)
        us.append(z * rs)
        vs.append(w * rs)
        zr = [sub(z, k) * rec[k] for k in range(8)]
        wr = [sub(w, k) * rec[k] for k in range(8)]
        for t in range(s + 1, n):
            qs = [lane(d[t], j0 + k) for k in range(8)]
            for k in range(8):
                yk = qs[k]
                for l in range(k):
                    yk = yk + m[k, l] * qs[l]
                d[t] = d[t] - yk * zr[k]
                e[t] = e[t] - yk * wr[k]
    return us, vs

def dot(a, b):
    return jnp.dot(a, b, precision=HI, preferred_element_type=F32)


def dot_t(a, b):
    return lax.dot_general(a, b, (((1,), (1,)), ((), ())), precision=HI, preferred_element_type=F32)


def tdot(a, b):
    return lax.dot_general(a, b, (((0,), (0,)), ((), ())), precision=HI, preferred_element_type=F32)

def factor(k_ref, u_ref, x_ref, w_ref, beside):
    for n, (i, j) in enumerate(UNITS):
        w_ref[B * i:B * i + B, B * j:B * j + B] = k_ref[B * n:B * n + B, :]
    x_ref[...] = jnp.zeros((NB, NB), F32)
    u_ref[...] = jnp.zeros((NB, NB), F32)
    row = lax.broadcasted_iota(jnp.int32, (8, B), 0)
    col = lax.broadcasted_iota(jnp.int32, (8, B), 1)
    for k in range(4):
        o = B * k
        d = [w_ref[o + 8 * t:o + 8 * t + 8, o:o + B] for t in range(16)]
        e = [jnp.where(col == row + 8 * t, 1.0, 0.0) for t in range(16)]
        us, vs = micro(d, e, lambda s, k=k: beside(k, s))
        for t in range(16):
            u_ref[o + 8 * t:o + 8 * t + 8, o:o + B] = jnp.where(col >= row + 8 * t, us[t], 0.0)
            x_ref[o + 8 * t:o + 8 * t + 8, o:o + B] = vs[t]
        li = x_ref[o:o + B, o:o + B]
        if k:
            x_ref[o:o + B, :o] = jnp.dot(li, x_ref[o:o + B, :o], precision=HI, preferred_element_type=F32)
        if k < 3:
            u = jnp.dot(li, w_ref[o:o + B, o + B:], precision=HI, preferred_element_type=F32)
            u_ref[o:o + B, o + B:] = u
            w_ref[o + B:, o + B:] = w_ref[o + B:, o + B:] - tdot(u, u)
            x_ref[o + B:, :o + B] = x_ref[o + B:, :o + B] - tdot(u, x_ref[o:o + B, :o + B])


def comm_kernel(
    g_ref, k_out, ap_out, aq_out, kbuf, ap, aq,
    lsem, ksend, krecv, asend, arecv, q1s, q1r, q2s, q2r, q3s, q3r, tok,
):
    r = lax.axis_index("row")
    q = lax.axis_index("col")
    x, zh, c = r // 4, (r // 2) % 2, r % 2
    zl, y = q // 4, q % 4
    z = zh * 8 + zl

    def dev(dx=0, dy=0, dz=0, dc=0):
        xx, yy, zz = (x + dx) % 4, (y + dy) % 4, (z + dz) % 16
        cc = (c + dc) % 2
        return {"row": xx * 4 + (zz // 8) * 2 + cc, "col": (zz % 8) * 4 + yy}

    ids = {}

    def near(**d):
        key = tuple(sorted((k, v) for k, v in d.items() if v))
        if key not in ids:
            ids[key] = dev(**d)
        return ids[key]

    group = [(dx, dc) for dx in range(4) for dc in range(2) if dx or dc]
    partners = [dict(dy=1), dict(dy=2), dict(dy=3), dict(dz=1), dict(dz=2), dict(dz=14), dict(dz=15)]
    partners += [dict(dx=dx, dc=dc) for dx, dc in group]
    for p in partners + [dict(dz=8)]:
        near(**p)
    barrier = pltpu.get_barrier_semaphore()
    for p in partners:
        pl.semaphore_signal(barrier, inc=1, device_id=near(**p), device_id_type=pl.DeviceIdType.MESH)

    kroot = (r == 0) & (q == 0)
    locals_k = [
        pltpu.make_async_copy(
            g_ref.at[pl.ds(B * i, B), pl.ds(B * j, B)], kbuf.at[pl.ds(B * n, B)], lsem.at[n]
        )
        for n, (i, j) in enumerate(UNITS)
    ]
    local_a = pltpu.make_async_copy(g_ref, ap, lsem.at[10])
    local_q = pltpu.make_async_copy(g_ref.at[pl.ds(0, NB)], aq, lsem.at[11])

    @pl.when(kroot)
    def _():
        for cp in locals_k:
            cp.start()

    @pl.when(q == 0)
    def _():
        local_a.start()

    @pl.when(r == 0)
    def _():
        local_q.start()

    pl.semaphore_wait(barrier, len(partners))

    @pl.when(kroot)
    def _():
        for cp in locals_k:
            cp.wait()

    @pl.when(q == 0)
    def _():
        local_a.wait()

    @pl.when(r == 0)
    def _():
        local_q.wait()

    def remote(ref, ssem, rsem, d):
        return pltpu.make_async_remote_copy(
            src_ref=ref, dst_ref=ref, send_sem=ssem, recv_sem=rsem,
            device_id=near(**d), device_id_type=pl.DeviceIdType.MESH,
        )

    pos = {"x": x, "y": y, "z": z}
    k_trees = []
    for order in ("xyz", "yzx", "zxy"):
        children = []
        for k, d in enumerate(order):
            head = c == 0
            for e in order[k + 1:]:
                head = head & (pos[e] == 0)
            v = pos[d]
            if d == "z":
                even = head & (v % 2 == 0)
                children.append((even & (v < 8), dict(dz=2)))
                children.append((even & (v < 8), dict(dz=1)))
                children.append((even & ((v == 0) | (v > 10)), dict(dz=14)))
                children.append((even & ((v == 0) | (v > 8)), dict(dz=15)))
            else:
                children += [(head & (v == 0), {"d" + d: n}) for n in (2, 1, 3)]
        children.append((c == 0, {"dc": 1}))
        k_trees.append(children)

    def k_chunk(ch):
        return kbuf.at[pl.ds(KCH * ch, KCH)]

    def k_round(s):
        for t in range(3):
            ch = 3 * s + t
            if ch >= KROWS // KCH:
                continue

            @pl.when(jnp.logical_not(kroot))
            def _():
                remote(k_chunk(ch), ksend.at[ch, 0], krecv.at[ch], {"dc": 1}).wait_recv()

            for n, (cond, d) in enumerate(k_trees[t]):
                @pl.when(cond)
                def _():
                    remote(k_chunk(ch), ksend.at[ch, n], krecv.at[ch], d).start()

    def q_piece(e):
        return aq.at[pl.ds(64 * e, 64)]

    mine = x * 2 + c

    @pl.when(r == 0)
    def _():
        for n, (dx, dc) in enumerate(group):
            remote(q_piece(dx * 2 + dc), q1s.at[n], q1r, dict(dx=dx, dc=dc)).start()

    def gather(n, dx, dc):
        to_source = (zh == 0) & ((x + dx) % 4 == 0) & ((c + dc) % 2 == 0)
        return jnp.logical_not(to_source), remote(
            q_piece(mine), q3s.at[n], q3r.at[mine], dict(dx=dx, dc=dc)
        )

    def q_cross():
        @pl.when(r != 0)
        def _():
            remote(q_piece(mine), q1s.at[0], q1r, dict(dc=1)).wait_recv()

        pl.semaphore_wait(tok.at[7], 1)
        remote(q_piece(mine), q2s, q2r, dict(dz=8)).start()
        for n, (dx, dc) in enumerate(group):
            cond, cp = gather(n, dx, dc)

            @pl.when(cond)
            def _():
                cp.start()

    def q_land():
        pl.semaphore_wait(tok.at[7], 1)
        remote(q_piece(mine), q2s, q2r, dict(dz=8)).wait_recv()
        for n, (dx, dc) in enumerate(group):
            gather(n, dx, dc)[1].start()

    def token(n):
        @pl.when(n > 0)
        def _():
            pl.semaphore_wait(tok.at[jnp.maximum(n - 1, 0)], 1)

        pl.semaphore_signal(
            tok.at[n], inc=1, device_id=near(dz=15), device_id_type=pl.DeviceIdType.MESH
        )

    a_trees = [
        [
            ((y == 0) & (zl < 7), dict(dz=1)),
            ((y == 0) & (zl >= 1), dict(dy=1)),
            (((y == 0) | (y == 3)) & (zl >= 1), dict(dy=3)),
            ((zl == 1) & (y != 0), dict(dz=15)),
        ],
        [
            ((y == 1) & (zl < 7), dict(dz=1)),
            (((y == 0) & (zl == 0)) | (y == 1) | (y == 2), dict(dy=1)),
            ((y == 1) & (zl >= 1), dict(dy=3)),
        ],
        [
            (((y == 3) | (y == 2)) & (zl < 7), dict(dz=1)),
            ((y == 3) & (zl >= 1), dict(dy=1)),
            (((y == 0) & (zl == 0)) | ((y == 3) & (zl == 0)) | (y == 2), dict(dy=3)),
        ],
    ]

    def a_chunk(ch):
        return ap.at[pl.ds(pl.multiple_of(ACH * ch, ACH), ACH)]

    def pick(options):
        value = options[-1][1]
        for cond, v in reversed(options[:-1]):
            value = jnp.where(cond, v, value)
        return value

    depths = [
        pick([((y == 0), zl), ((zl == 0) & (y == 2), 4), (zl == 0, 3), (y == 2, zl + 2), (True, zl + 1)]),
        pick([((y == 0) & (zl == 0), 0), (y == 1, zl + 1), (y == 3, zl + 3), (True, zl + 2)]),
        pick([((y == 0) & (zl == 0), 0), (y == 3, zl + 1), (y == 1, zl + 3), (True, zl + 2)]),
    ]

    def a_step(g, carry):
        for t in range(3):
            k = g - LAG * depths[t]
            ch = 3 * k + t

            @pl.when((k >= 0) & (ch < NA))
            def _():
                @pl.when(q != 0)
                def _():
                    remote(a_chunk(ch), asend.at[ch, 0], arecv.at[ch], dict(dy=1)).wait_recv()

                for n, (cond, d) in enumerate(a_trees[t]):
                    @pl.when(cond)
                    def _():
                        remote(a_chunk(ch), asend.at[ch, n], arecv.at[ch], d).start()

        @pl.when((g >= TOKEN) & (g < TOKEN + 8))
        def _():
            token(g - TOKEN)

        @pl.when((g == CROSS) & (zh == 0))
        def _():
            q_cross()

        @pl.when((g == LAND) & (zh == 1))
        def _():
            q_land()

        return carry

    chunks = -(-NA // 3)
    steps = max(chunks + 10 * LAG, LAND + 1)
    far = jnp.minimum(x, 4 - x) + jnp.minimum(y, 4 - y) + jnp.minimum(z, 16 - z)
    early = FIRST + (far * EARLY) // 8
    lax.fori_loop(0, early, a_step, 0)
    rounds = -(-(KROWS // KCH) // 3)
    for s in range(rounds):
        k_round(s)
        a_step(early + s, 0)

    lax.fori_loop(early + rounds, steps, a_step, 0)

    for n, (dx, dc) in enumerate(group):
        e = ((x + dx) % 4) * 2 + (c + dc) % 2
        cond, cp = gather(n, dx, dc)

        @pl.when(r != 0)
        def _():
            remote(q_piece(e), q3s.at[n], q3r.at[e], dict(dc=1)).wait_recv()

        @pl.when(cond)
        def _():
            cp.wait_send()

        @pl.when(r == 0)
        def _():
            remote(q_piece(dx * 2 + dc), q1s.at[n], q1r, dict(dx=dx, dc=dc)).wait_send()

    @pl.when(zh == 0)
    def _():
        remote(q_piece(mine), q2s, q2r, dict(dz=8)).wait_send()

    for ch in range(KROWS // KCH):
        for n, (cond, d) in enumerate(k_trees[ch % 3]):
            @pl.when(cond)
            def _():
                remote(k_chunk(ch), ksend.at[ch, n], krecv.at[ch], d).wait_send()

    def a_drain(k, carry):
        for t in range(3):
            ch = 3 * k + t

            @pl.when(ch < NA)
            def _():
                for n, (cond, d) in enumerate(a_trees[t]):
                    @pl.when(cond)
                    def _():
                        remote(a_chunk(ch), asend.at[ch, n], arecv.at[ch], d).wait_send()

        return carry

    lax.fori_loop(0, chunks, a_drain, 0)

    outs = [
        pltpu.make_async_copy(src, dst, lsem.at[n])
        for n, (src, dst) in enumerate([(kbuf, k_out), (ap, ap_out), (aq, aq_out)])
    ]
    for cp in outs:
        cp.start()
    for cp in outs:
        cp.wait()


def distribute(kernel):
    dma, vmem = pltpu.SemaphoreType.DMA, pltpu.VMEM
    square = (NB, NB)
    return pl.pallas_call(
        comm_kernel,
        out_shape=[
            jax.ShapeDtypeStruct((KROWS, B), F32),
            jax.ShapeDtypeStruct((2 * NB, NB), F32),
            jax.ShapeDtypeStruct(square, F32),
        ],
        in_specs=[pl.BlockSpec(memory_space=pl.ANY)],
        out_specs=[pl.BlockSpec(memory_space=pl.ANY)] * 3,
        scratch_shapes=[
            vmem((KROWS, B), F32), vmem((2 * NB, NB), F32), vmem(square, F32),
            dma((12,)),
            dma((KROWS // KCH, 11)), dma((KROWS // KCH,)),
            dma((NA, 4)), dma((NA,)),
            dma((7,)), dma(()),
            dma(()), dma(()),
            dma((7,)), dma((8,)),
            pltpu.SemaphoreType.REGULAR((8,)),
        ],
        compiler_params=pltpu.CompilerParams(collective_id=0, has_side_effects=True),
        name="distribute",
    )(kernel)


def update_kernel(k_any, a_any, q_any, g_any, o_ref, kbuf, ap, aq, u_ref, x_ref, w_ref, pq, p_ref, sems):
    r = lax.axis_index("row")
    q = lax.axis_index("col")
    loads = [
        pltpu.make_async_copy(src, dst, sems.at[n])
        for n, (src, dst) in enumerate([(k_any, kbuf), (a_any, ap), (q_any, aq), (g_any, o_ref)])
    ]
    for cp in loads:
        cp.start()
    loads[0].wait()

    def beside(k, s):
        if k == 0:
            return
        if k == 1 and s == 0:
            loads[1].wait()
            loads[2].wait()
        lo, hi = B * (k - 1), B * k
        part = slice(64 * s, 64 * s + 64)
        p_ref[part, lo:hi] = dot_t(ap[part, :hi], x_ref[lo:hi, :hi])
        if s < 4:
            cols = slice(B * s, B * s + B)
            pq[lo:hi, cols] = dot(x_ref[lo:hi, :hi], aq[:hi, cols])

    factor(kbuf, u_ref, x_ref, w_ref, beside)
    loads[3].wait()
    last = NB - B
    pq[last:] = dot(x_ref[last:, :], aq[...])
    rows = 256

    def body(n, carry):
        sl = pl.ds(pl.multiple_of(rows * n, rows), rows)
        p = jnp.concatenate([p_ref[sl, :last], dot_t(ap[sl, :], x_ref[last:, :])], axis=1)

        @pl.when(q == 0)
        def _():
            o_ref[sl, :] = p

        @pl.when(q != 0)
        def _():
            o_ref[sl, :] = o_ref[sl, :] - dot(p, pq[...])

        return carry

    lax.fori_loop(0, 2 * NB // rows, body, 0)

    @pl.when(r == 0)
    def _():
        @pl.when(q == 0)
        def _():
            for i in range(4):
                for j in range(4):
                    o_ref[B * i:B * i + B, B * j:B * j + B] = u_ref[B * j:B * j + B, B * i:B * i + B].T

        @pl.when(q != 0)
        def _():
            o_ref[:NB, :] = jnp.zeros((NB, NB), F32)


def update(kbuf, ap, aq, kernel):
    vmem = pltpu.VMEM
    return pl.pallas_call(
        update_kernel,
        out_shape=jax.ShapeDtypeStruct((2 * NB, NB), F32),
        in_specs=[pl.BlockSpec(memory_space=pl.ANY)] * 4,
        out_specs=pl.BlockSpec(memory_space=vmem),
        scratch_shapes=[
            vmem((KROWS, B), F32), vmem((2 * NB, NB), F32), vmem((NB, NB), F32),
            vmem((NB, NB), F32), vmem((NB, NB), F32), vmem((NB, NB), F32), vmem((NB, NB), F32),
            vmem((2 * NB, NB), F32), pltpu.SemaphoreType.DMA((4,)),
        ],
        name="update",
    )(kbuf, ap, aq, kernel)


def on_device(kernel):
    kbuf, ap, aq = distribute(kernel)
    return update(kbuf, ap, aq, kernel)


def solution(mesh):
    return jax.shard_map(
        on_device, mesh=mesh, in_specs=(P("row", "col"),), out_specs=P("row", "col"), check_vma=False
    )
```
